32 devices in a mesh: dp: 8 (over z, y), mp: 4 (over x, core).
Axes of the slice: x: 2, y: 2, z: 4, core: 2. Of those that a mesh axis runs over, the one named last changes fastest.
Arguments:
- query_states: bfloat16 [128, 8, 8192], P(None, 'dp', 'mp'), may hold values from -6 to 6
- key_states: bfloat16 [128, 8, 1024], P(None, 'dp', 'mp'), may hold values from -6 to 6
- value_state_array: bfloat16 [128, 8, 1024], P(None, 'dp', 'mp'), may hold values from -6 to 6
- grad_output: bfloat16 [128, 8, 8192], P(None, 'dp', 'mp'), may hold values from -6 to 6
- doc_lengths: int32 [8], P('dp'), may hold values from 1 to 256, as said below
Outputs:
- attention: bfloat16 [128, 8, 8192], P(None, 'dp', 'mp')
- query_grad: bfloat16 [128, 8, 8192], P(None, 'dp', 'mp')
- key_grad: bfloat16 [128, 8, 1024], P(None, 'dp', 'mp')
- value_grad: bfloat16 [128, 8, 1024], P(None, 'dp', 'mp')
The draws below stay inside these ranges and needn't reach their ends.
Inputs may be any that keep to these rules, and one draw needn't show every extreme that they name: `doc_lengths`: every length is positive, the lengths sum to 1024, and the longest document has exactly 256 tokens.
All inputs are finite; a program needn't handle non-finite values.
Results may differ from the reference program's by a relative error of at most 0.025.
Values may be sent and summed in bfloat16 or wider, within the bound.
A program may use at most 64 MiB of HBM per device.

```python
import jax
import jax.numpy as jnp
from jax import lax

QUERY_HEADS = 64
KEY_VALUE_HEADS = 8
HEAD_SIZE = 128
TOKENS_PER_ROW = 128
N_DP = 8


def draw_doc_lengths(key, part):
    token_count = TOKENS_PER_ROW * N_DP
    slot_capacity = 2 * TOKENS_PER_ROW
    first_key, second_key = jax.random.split(jax.random.fold_in(key, 5))
    owners = jnp.arange(N_DP, dtype=jnp.int32)
    chosen = jax.random.randint(second_key, (), 0, N_DP)
    weights = jnp.where(owners == chosen, 0, jax.random.randint(first_key, (N_DP,), 3, 7))
    spread = token_count - slot_capacity
    shares = spread * weights // jnp.sum(weights)
    leftover = spread - jnp.sum(shares)
    others = (owners != chosen).astype(jnp.int32)
    order_rank = jnp.cumsum(others) - 1
    shares = shares + jnp.where((others == 1) & (order_rank < leftover), 1, 0)
    return jnp.where(owners == chosen, slot_capacity, shares).astype(jnp.int32)


def draw_query_states(key, part):
    window_layout = (TOKENS_PER_ROW, N_DP, QUERY_HEADS * HEAD_SIZE)
    noise_key = jax.random.fold_in(key, 21)
    return jnp.clip(jax.random.normal(noise_key, window_layout), -4.0, 4.0).astype(jnp.bfloat16)


def draw_key_states(key, part):
    window_layout = (TOKENS_PER_ROW, N_DP, KEY_VALUE_HEADS * HEAD_SIZE)
    noise_key = jax.random.fold_in(key, 22)
    return jnp.clip(jax.random.normal(noise_key, window_layout), -4.0, 4.0).astype(jnp.bfloat16)


def block_levels(key, dims, pieces, least, top_value):
    factor_of, own = 1.0, jax.random.fold_in(key, 6)
    for axis_at, blocks in pieces:
        draws = jnp.exp(jax.random.uniform(jax.random.fold_in(own, axis_at), (blocks,), jnp.float32, least / len(pieces), top_value / len(pieces)))
        factor_of = factor_of * jnp.repeat(draws, dims[axis_at] // blocks).reshape([-1 if axis == axis_at else 1 for axis in range(len(dims))])
    return factor_of


def centred(rng, extent, width, bound, cuts=(), held_as=jnp.bfloat16):
    values = jax.random.normal(rng, extent, jnp.float32) * width
    if len(cuts) > 0:
        values = block_levels(rng, extent, cuts, -0.22, 0.18) * values
    return jnp.clip(values, min=-bound, max=bound).astype(held_as)


def setup_inputs(seed: int = 0) -> dict:
    splits = jax.random.split(jax.random.key(seed), 6)
    return {
        "query_states": draw_query_states(jax.random.fold_in(splits[5], 71), 0),
        "key_states": draw_key_states(jax.random.fold_in(splits[5], 71), 0),
        "value_state_array": centred(splits[2], (TOKENS_PER_ROW, N_DP, KEY_VALUE_HEADS * HEAD_SIZE), 1.0, 6.0, ((1, 8), (2, 4))),
        "grad_output": centred(splits[3], (TOKENS_PER_ROW, N_DP, QUERY_HEADS * HEAD_SIZE), 1.0, 6.0, ((1, 8), (2, 4))),
        "doc_lengths": draw_doc_lengths(jax.random.fold_in(splits[5], 71), 0),
    }


def contract(form, first, second):
    return jnp.einsum(form, first.astype(jnp.float32), second.astype(jnp.float32))


def forward_tile(query_rows, key_row_block, value_row_block, length, first_row):
    scaling = query_rows.shape[-1] ** -0.5
    row_place = first_row + jnp.arange(query_rows.shape[0], dtype=jnp.int32)
    key_place = jnp.arange(key_row_block.shape[0], dtype=jnp.int32)
    allowed = (key_place[None, :] <= row_place[:, None]) & (key_place[None, :] < length)
    scores = contract("qhge,khe->hgqk", query_rows, key_row_block) * scaling
    scores = jnp.where(allowed, scores, -1e30)
    row_max = jnp.max(scores, axis=-1, keepdims=True)
    raised = jnp.exp(scores - row_max)
    attn_weights = raised / jnp.sum(raised, axis=-1, keepdims=True)
    attn_weights = jnp.where((row_place < length)[:, None], attn_weights, 0.0)
    rounded = attn_weights.astype(jnp.bfloat16)
    attended = contract("hgqk,khe->qhge", rounded, value_row_block).astype(jnp.bfloat16)
    return attended, attn_weights, rounded


def backward_tile(query_rows, key_row_block, value_row_block, gradient_row_block, attended, attn_weights, rounded):
    scaling = query_rows.shape[-1] ** -0.5
    dprobs = contract("qhge,khe->hgqk", gradient_row_block, value_row_block)
    row_dot = jnp.sum(gradient_row_block.astype(jnp.float32) * attended.astype(jnp.float32), axis=-1)
    row_dot = jnp.transpose(row_dot, (1, 2, 0))[..., None]
    dscores = (attn_weights * (dprobs - row_dot)).astype(jnp.bfloat16)
    dquery = (contract("hgqk,khe->qhge", dscores, key_row_block) * scaling).astype(jnp.bfloat16)
    key_total = contract("hgqk,qhge->khe", dscores, query_rows) * scaling
    value_total = contract("hgqk,qhge->khe", rounded, gradient_row_block)
    return dquery, key_total, value_total


def reference(query_states, key_states, value_state_array, grad_output, doc_lengths):
    token_count = TOKENS_PER_ROW * N_DP
    slot_capacity = 2 * TOKENS_PER_ROW
    query_group = QUERY_HEADS // KEY_VALUE_HEADS

    def padded(states):
        flat = states.reshape(token_count, states.shape[-1])
        return jnp.concatenate([flat, jnp.zeros((slot_capacity, flat.shape[-1]), flat.dtype)], axis=0)

    query_flattened = padded(query_states)
    key_flattened = padded(key_states)
    value_flattened = padded(value_state_array)
    gradient_flattened = padded(grad_output)
    starts = (jnp.cumsum(doc_lengths) - doc_lengths).astype(jnp.int32)
    written = (jnp.zeros_like(query_flattened), jnp.zeros_like(query_flattened), jnp.zeros_like(key_flattened), jnp.zeros_like(key_flattened))

    def advance(written, owner_index):
        doc_start = starts[owner_index]
        length = doc_lengths[owner_index]

        def packed_window(flat):
            return lax.dynamic_slice_in_dim(flat, doc_start, slot_capacity, 0)

        query_rows = packed_window(query_flattened).reshape(slot_capacity, KEY_VALUE_HEADS, query_group, HEAD_SIZE)
        key_row_block = packed_window(key_flattened).reshape(slot_capacity, KEY_VALUE_HEADS, HEAD_SIZE)
        value_row_block = packed_window(value_flattened).reshape(slot_capacity, KEY_VALUE_HEADS, HEAD_SIZE)
        gradient_row_block = packed_window(gradient_flattened).reshape(slot_capacity, KEY_VALUE_HEADS, query_group, HEAD_SIZE)
        attended, attn_weights, rounded = forward_tile(query_rows, key_row_block, value_row_block, length, 0)
        dquery, key_total, value_total = backward_tile(query_rows, key_row_block, value_row_block, gradient_row_block, attended, attn_weights, rounded)
        results = (attended.reshape(slot_capacity, -1), dquery.reshape(slot_capacity, -1),
                   key_total.astype(jnp.bfloat16).reshape(slot_capacity, -1),
                   value_total.astype(jnp.bfloat16).reshape(slot_capacity, -1))
        inside = jnp.arange(slot_capacity, dtype=jnp.int32) < length
        updated = tuple(
            lax.dynamic_update_slice_in_dim(before, jnp.where(inside[:, None], computed, packed_window(before)), doc_start, 0)
            for before, computed in zip(written, results))
        return updated, None

    written, _ = lax.scan(advance, written, jnp.arange(N_DP, dtype=jnp.int32))
    return (written[0][:token_count].reshape(TOKENS_PER_ROW, N_DP, -1),
            written[1][:token_count].reshape(TOKENS_PER_ROW, N_DP, -1),
            written[2][:token_count].reshape(TOKENS_PER_ROW, N_DP, -1),
            written[3][:token_count].reshape(TOKENS_PER_ROW, N_DP, -1))
```

```python
import jax
import jax.numpy as jnp
from jax import lax
from jax.experimental import pallas as pl
from jax.experimental.pallas import tpu as pltpu
from jax.sharding import PartitionSpec as P

QUERY_HEADS = 64
KEY_VALUE_HEADS = 8
HEAD_SIZE = 128


def contract(form, first, second):
    return jnp.einsum(form, first, second, preferred_element_type=jnp.float32)


def forward_tile(query_rows, key_row_block, value_row_block, length, first_row):
    scaling = query_rows.shape[-1] ** (-0.5)
    row_place = first_row + jnp.arange(query_rows.shape[0], dtype=jnp.int32)
    key_place = jnp.arange(key_row_block.shape[0], dtype=jnp.int32)
    allowed = (key_place[None, :] <= row_place[:, None]) & (key_place[None, :] < length)
    scores = contract("qhge,khe->hgqk", query_rows, key_row_block) * scaling
    scores = jnp.where(allowed, scores, -1e30)
    row_max = jnp.max(scores, axis=-1, keepdims=True)
    raised = jnp.exp(scores - row_max)
    attn_weights = raised / jnp.sum(raised, axis=-1, keepdims=True)
    attn_weights = jnp.where((row_place < length)[:, None], attn_weights, 0.0)
    rounded = attn_weights.astype(jnp.bfloat16)
    attended = contract("hgqk,khe->qhge", rounded, value_row_block).astype(jnp.bfloat16)
    return (attended, attn_weights, rounded)


def backward_tile(
    query_rows, key_row_block, value_row_block, gradient_row_block, attended, attn_weights, rounded
):
    scaling = query_rows.shape[-1] ** (-0.5)
    dprobs = contract("qhge,khe->hgqk", gradient_row_block, value_row_block)
    row_dot = jnp.sum(
        gradient_row_block.astype(jnp.float32) * attended.astype(jnp.float32), axis=-1
    )
    row_dot = jnp.transpose(row_dot, (1, 2, 0))[..., None]
    dscores = (attn_weights * (dprobs - row_dot)).astype(jnp.bfloat16)
    dquery = (contract("hgqk,khe->qhge", dscores, key_row_block) * scaling).astype(jnp.bfloat16)
    key_total = contract("hgqk,qhge->khe", dscores, query_rows) * scaling
    value_total = contract("hgqk,qhge->khe", rounded, gradient_row_block)
    return (dquery, key_total, value_total)


def per_device_by_document(query_states, key_states, value_state_array, grad_output, doc_lengths):
    shards = lax.axis_size("dp")
    source = lax.axis_index("dp")
    lengths = lax.all_gather(doc_lengths, "dp", axis=0, tiled=True)
    owners = jnp.arange(shards, dtype=jnp.int32)
    starts = jnp.sum(jnp.where(owners[None, :] < owners[:, None], lengths[None, :], 0), axis=1)
    row_count = query_states.shape[0]
    slot_capacity = 2 * row_count
    per_peer = slot_capacity // shards
    kv_heads = key_states.shape[-1] // HEAD_SIZE
    query_group = QUERY_HEADS // KEY_VALUE_HEADS
    places = jnp.arange(per_peer, dtype=jnp.int32)
    offsets = jnp.mod(source - starts, shards)
    within = places[:, None] * shards + offsets[None, :]
    sendable = within < lengths[None, :]
    local_rows = jnp.where(sendable, (starts[None, :] + within - source) // shards, -1)
    my_start = jnp.sum(jnp.where(owners == source, starts, 0))
    my_length = jnp.sum(jnp.where(owners == source, lengths, 0))
    token_ids = jnp.arange(row_count, dtype=jnp.int32) * shards + source
    begun = starts[None, :] <= token_ids[:, None]
    owner_index = jnp.sum(begun.astype(jnp.int32), axis=1) - 1
    home_slot = token_ids - jnp.max(jnp.where(begun, starts[None, :], 0), axis=1)
    home_index = home_slot // shards * shards + owner_index

    def pick(index, flat):
        chosen = index[:, None] == jnp.arange(flat.shape[0], dtype=jnp.int32)[None, :]
        return contract("ij,jk->ik", chosen.astype(flat.dtype), flat).astype(flat.dtype)

    def pack_rows(states):
        flat = states[:, 0, :]
        return pick(local_rows.reshape(-1), flat).reshape(per_peer, shards, flat.shape[-1])

    def arrive(received):
        rolled = jnp.roll(received, -my_start, axis=1)
        return rolled.reshape(slot_capacity, received.shape[-1])

    def as_queries(flat):
        return flat.reshape(slot_capacity, kv_heads, query_group, HEAD_SIZE)

    def as_keys(flat):
        return flat.reshape(slot_capacity, kv_heads, HEAD_SIZE)

    def depart(slots):
        return jnp.roll(slots.reshape(per_peer, shards, -1), my_start, axis=1)

    def settle(received):
        flat = received.reshape(slot_capacity, received.shape[-1])
        return pick(home_index, flat)[:, None, :]

    spans = [(0, slot_capacity, slot_capacity)]
    arrived = (
        lax.all_to_all(pack_rows(query_states), "dp", split_axis=1, concat_axis=1, tiled=True),
        lax.all_to_all(pack_rows(key_states), "dp", split_axis=1, concat_axis=1, tiled=True),
        lax.all_to_all(pack_rows(value_state_array), "dp", split_axis=1, concat_axis=1, tiled=True),
    )
    query_rows = as_queries(arrive(arrived[0]))
    key_row_block = as_keys(arrive(arrived[1]))
    value_row_block = as_keys(arrive(arrived[2]))
    first_row, row_span, key_reach = spans[0]

    def compute(first_row=first_row, row_span=row_span, key_reach=key_reach):
        return forward_tile(query_rows, key_row_block, value_row_block, my_length, first_row)

    pieces = [compute()]
    attended = jnp.concatenate([piece[0] for piece in pieces], axis=0)
    output_home = lax.all_to_all(depart(attended), "dp", split_axis=1, concat_axis=1, tiled=True)
    grad_arrived = lax.all_to_all(
        pack_rows(grad_output), "dp", split_axis=1, concat_axis=1, tiled=True
    )
    gradient_row_block = as_queries(arrive(grad_arrived))
    query_parts = []
    key_total = jnp.zeros((slot_capacity, kv_heads, HEAD_SIZE), jnp.float32)
    value_total = jnp.zeros((slot_capacity, kv_heads, HEAD_SIZE), jnp.float32)
    for (first_row, row_span, key_reach), piece in zip(spans, pieces):

        def compute(first_row=first_row, row_span=row_span, key_reach=key_reach, piece=piece):
            return backward_tile(
                query_rows,
                key_row_block,
                value_row_block,
                gradient_row_block,
                piece[0],
                piece[1],
                piece[2],
            )

        result = compute()
        query_parts.append(result[0])
        key_total = key_total.at[:key_reach].add(result[1])
        value_total = value_total.at[:key_reach].add(result[2])
    dquery = query_parts[0]
    dquery, key_part, value_part = (
        dquery,
        key_total.astype(jnp.bfloat16),
        value_total.astype(jnp.bfloat16),
    )
    returned = (
        lax.all_to_all(depart(dquery), "dp", split_axis=1, concat_axis=1, tiled=True),
        lax.all_to_all(depart(key_part), "dp", split_axis=1, concat_axis=1, tiled=True),
        lax.all_to_all(depart(value_part), "dp", split_axis=1, concat_axis=1, tiled=True),
    )
    return (settle(output_home), settle(returned[0]), settle(returned[1]), settle(returned[2]))


MESH = pl.DeviceIdType.MESH
LOG2E = 1.4426950408889634
SPAN = 256
PAIR = 2
LINE = 4
STEPS = (
    (
        "s2004", "s0002", "s3001", "s1002", "s0004", "s2002", "s3004", "s0003", "s0001", "s1004", "s0011", "s1001",
        "s2104", "s1011", "s3011", "s0104", "s2011", "s0204", "s0304", "s2001", "s1204", "s3204", "c00", "c01",
        "c10", "c11", "p03", "p02", "p01", "c20", "c21", "p12", "p11", "c30", "l03", "p13",
        "c31", "p31", "l02", "p33", "p22", "l01", "p23", "l12", "p32", "l11", "p21", "p20",
        "l13", "p00", "l31", "l33", "p10", "l22", "l23", "l32", "p30", "l21", "e0", "e1",
        "e3", "e2",
    ),
    (
        "s0102", "s3100", "s1102", "s1100", "s1104", "s2100", "s0100", "s0104", "s2104", "s3104", "s0204", "s0200",
        "s1204", "s3002", "s0304", "s2112", "s1110", "s1304", "s1200", "s2102", "s3112", "s1300", "s2300", "s3103",
        "s2304", "c00", "c01", "s1310", "s3102", "s3304", "s2210", "c10", "s2310", "c11", "p03", "s2200",
        "p02", "s3110", "p00", "s3300", "c20", "c21", "p12", "s3310", "p13", "c30", "c31", "p32",
        "p10", "l02", "l03", "p33", "l12", "p22", "p23", "l13", "l32", "l00", "p20", "l10",
        "p01", "l33", "p11", "l22", "p31", "p30", "l23", "l20", "p21", "l30", "e0", "e1",
        "e2", "e3",
    ),
)

def attend(refs, me, band, head, mask, group):
    kv, q_buf, g_buf, attn_ref, dq_ref, total = refs
    shards, rows = kv.shape[1], kv.shape[3]
    first = max(band - 1, 0)
    keys = (band - first + 1) * shards * rows
    scale = HEAD_SIZE**-0.5
    lanes = pl.ds(head * HEAD_SIZE, HEAD_SIZE)
    here = pl.ds(band * rows, rows)

    def stack(buf):
        base = head * group
        return jnp.concatenate(
            [buf[here, pl.ds((base + g) * HEAD_SIZE, HEAD_SIZE)] for g in range(group)], axis=0
        )

    def dot(first_one, second_one, dims):
        return lax.dot_general(
            first_one, second_one, (dims, ((), ())), preferred_element_type=jnp.float32
        )

    key_rows = kv[first : band + 1, :, 0, :, lanes].reshape(keys, HEAD_SIZE)
    value_rows = kv[first : band + 1, :, 1, :, lanes].reshape(keys, HEAD_SIZE)
    query = stack(q_buf)
    grad = stack(g_buf)
    scores = jnp.where(mask, dot(key_rows, query, ((1,), (1,))), -1e30)
    dprobs = dot(value_rows, grad, ((1,), (1,)))
    top = jnp.max(scores, axis=0, keepdims=True)
    raised = jnp.exp2((scores - top) * (scale * LOG2E))
    probs = raised * (1.0 / jnp.sum(raised, axis=0, keepdims=True))
    low = probs.astype(jnp.bfloat16)
    weighted = probs * dprobs
    delta = jnp.sum(weighted, axis=0, keepdims=True)
    dscores = (weighted - probs * delta).astype(jnp.bfloat16)
    attended = dot(value_rows, low, ((0,), (0,))).T.astype(jnp.bfloat16)
    dquery = (dot(key_rows, dscores, ((0,), (0,))) * scale).T.astype(jnp.bfloat16)
    for g in range(group):
        columns = pl.ds((head * group + g) * HEAD_SIZE, HEAD_SIZE)
        attn_ref[here, columns] = attended[g * rows : (g + 1) * rows]
        dq_ref[here, columns] = dquery[g * rows : (g + 1) * rows]
    parts = (dot(dscores, query, ((1,), (0,))), dot(low, grad, ((1,), (0,))))
    size = shards * rows
    for kind, part in enumerate(parts):
        if first < band:
            total[first, :, kind, :, lanes] += part[:size].reshape(shards, rows, HEAD_SIZE)
        total[band, :, kind, :, lanes] = part[keys - size :].reshape(shards, rows, HEAD_SIZE)


def local_kernel(
    len_ref, q_hbm, k_hbm, v_hbm, g_hbm, attn_ref, dq_ref, dk_ref, dv_ref,
    lens, kv, q_buf, g_buf, total, pair_out, pair_in, line_out, line_in,
    local_sem, len_send, len_recv, kv_send, kv_recv,
    pair_sum_send, pair_sum_recv, line_sum_send, line_sum_recv,
):
    me = lax.axis_index("dp")
    bands, shards, _, rows, width = kv.shape
    heads = width // HEAD_SIZE
    group = q_buf.shape[1] // width
    length = shards // PAIR
    y = lax.rem(me, PAIR)
    z = lax.div(me, PAIR)
    slot = y * length + z
    partner = z * PAIR + 1 - y
    peers = [lax.rem(me + o, shards) for o in range(1, shards)]

    def push(src, dst, send, recv, peer):
        return pltpu.make_async_remote_copy(
            src_ref=src, dst_ref=dst, send_sem=send, recv_sem=recv,
            device_id={"dp": peer}, device_id_type=MESH,
        )

    loads = [
        pltpu.make_async_copy(k_hbm, kv.at[:, slot, 0], local_sem.at[0]),
        pltpu.make_async_copy(v_hbm, kv.at[:, slot, 1], local_sem.at[1]),
        pltpu.make_async_copy(q_hbm, q_buf, local_sem.at[2]),
        pltpu.make_async_copy(g_hbm, g_buf, local_sem.at[3]),
    ]
    for load in loads:
        load.start()
    barrier = pltpu.get_barrier_semaphore()
    for peer in peers:
        pl.semaphore_signal(barrier, inc=1, device_id={"dp": peer}, device_id_type=MESH)
    lens[me] = jnp.full(lens.shape[1:], len_ref[0], jnp.int32)
    pl.semaphore_wait(barrier, shards - 1)
    sends = []
    moves = [[] for _ in range(length)]
    known = [set() for _ in range(length)]

    def go(copy):
        copy.start()
        sends.append(copy)

    def edge(k):
        return k in (0, length - 1)

    def there(rel, s):
        return (y if rel == 0 else 1 - y) * length + s

    def piece(band, rel, s):
        return kv.at[band, there(rel, s)]

    def sending(at, band, rel, s, target):
        over = target == length
        return push(
            piece(band, rel, s), piece(band, rel, s), kv_send.at[at],
            kv_recv.at[band, (1 - rel if over else rel) * length + s],
            partner if over else target * PAIR + y,
        )

    def arrived(k, band, rel, s):
        if (rel, s) != (0, k) and (band, rel, s) not in known[k]:
            known[k].add((band, rel, s))
            push(
                piece(band, rel, s), piece(band, rel, s), kv_send.at[0],
                kv_recv.at[band, rel * length + s], partner,
            ).wait_recv()

    def each(body):
        for k in range(length):
            pl.when(z == k)(lambda k=k: body(k))

    def across(band, s):
        return push(
            pair_out.at[band, s], pair_in.at[band, s],
            pair_sum_send.at[band, s], pair_sum_recv.at[band, s], partner,
        )

    def along(band, source, target):
        return push(
            line_out.at[band, target], line_in.at[band, source],
            line_sum_send.at[band, target], line_sum_recv.at[band, source], target * PAIR + y,
        )

    def relay(k, band, s, rel, target):
        arrived(k, band, rel, s)
        sending(len(moves[k]), band, rel, s, target).start()
        moves[k].append((band, rel, s, target))

    def pair_sum(k, band, s):
        pair_out[band, s] = total[band, there(1, s)].astype(jnp.bfloat16)
        across(band, s).start()

    def line_sum(k, band, s):
        across(band, s).wait_recv()
        both = total[band, there(0, s)] + pair_in[band, s].astype(jnp.float32)
        line_out[band, s] = both.astype(jnp.bfloat16)
        along(band, k, s).start()

    def drain(k):
        for at, which in enumerate(moves[k]):
            sending(at, *which).wait_send()
        for band in range(bands):
            for s in range(length):
                across(band, s).wait_send()
                if s != k:
                    along(band, k, s).wait_send()

    def finish(k, band):
        across(band, k).wait_recv()
        sums = total[band, there(0, k)] + pair_in[band, k].astype(jnp.float32)
        for s in range(length):
            if s == k:
                continue
            along(band, s, k).wait_recv()
            sums = sums + line_in[band, s].astype(jnp.float32)
        here = pl.ds(band * rows, rows)
        dk_ref[here, :] = (sums[0] * HEAD_SIZE**-0.5).astype(jnp.bfloat16)
        dv_ref[here, :] = sums[1].astype(jnp.bfloat16)

    for at, peer in enumerate(peers):
        go(push(lens.at[me], lens.at[me], len_send.at[at], len_recv.at[me], peer))
    loads[0].wait()
    loads[1].wait()
    columns = group * rows
    lane_row = lax.rem(lax.broadcasted_iota(jnp.int32, (1, columns), 1), rows)
    starts = []

    def documents():
        for at, peer in enumerate(peers):
            push(
                lens.at[peer], lens.at[peer], len_send.at[at], len_recv.at[peer], peer
            ).wait_recv()
        running = jnp.zeros((1, lens.shape[-1]), jnp.int32)
        for b in range(shards):
            starts.append(jnp.concatenate([running] * (columns // lens.shape[-1]), axis=1))
            running = running + lens[b, 0:1, :]
        loads[2].wait()
        loads[3].wait()

    def compute(band, head):
        first = max(band - 1, 0)
        if head == 0:
            token = (band * rows + lane_row) * shards + me
            begin_at = jnp.zeros_like(token)
            for s in starts:
                begin_at = jnp.where(s <= token, s, begin_at)
            block = (band - first + 1, PAIR, length, rows, columns)
            iota = [lax.broadcasted_iota(jnp.int32, block, axis) for axis in range(4)]
            key_row = (first + iota[0]) * rows + iota[3]
            key_token = (key_row * shards + iota[2] * PAIR + iota[1]).reshape(-1, columns)
            masks[band] = (key_token <= token) & (key_token >= begin_at)
            each(lambda k: [arrived(k, band, rel, s) for rel in (0, 1) for s in range(length)] and None)
        attend((kv, q_buf, g_buf, attn_ref, dq_ref, total), me, band, head, masks[band], group)

    def act(k, step):
        kind, band, *which = step[0], *(int(digit) for digit in step[1:])
        flip = (lambda at: length - 1 - at) if k >= length // 2 else (lambda at: at)
        if kind == "s":
            s, rel, target = which
            relay(k, band, flip(s), rel, target if target == length else flip(target))
        elif kind == "p":
            pair_sum(k, band, flip(which[0]))
        elif kind == "l":
            line_sum(k, band, flip(which[0]))
        else:
            finish(k, band)

    masks = {}
    queues = [list(STEPS[0 if edge(k) else 1]) for k in range(length)]

    def pump(k):
        while queues[k] and queues[k][0][0] != "c":
            act(k, queues[k].pop(0))

    def begin(k):
        while queues[k][0][0] == "s" and queues[k][0][2:4] == ("00" if edge(k) else "10"):
            act(k, queues[k].pop(0))

    each(begin)
    while True:
        each(pump)
        if not queues[0]:
            break
        if not starts:
            documents()
        step = queues[0][0]
        for queue in queues:
            queue.pop(0)
        compute(int(step[1]), int(step[2]))
    for send in sends:
        send.wait_send()
    each(drain)


def hand_over(*refs):
    count = len(refs) // 2
    sems = refs[-1]
    copies = [
        pltpu.make_async_copy(refs[at], refs[count + at], sems.at[at]) for at in range(count)
    ]
    for copy in copies:
        copy.start()
    for copy in copies:
        copy.wait()


def per_device(query_states, key_states, value_state_array, grad_output, doc_lengths):
    shards = lax.axis_size("dp")
    row_count = query_states.shape[0]
    rows = SPAN // shards
    if rows % 16 or row_count % rows or shards != PAIR * LINE:
        return per_device_by_document(
            query_states, key_states, value_state_array, grad_output, doc_lengths
        )
    bands = row_count // rows
    width = key_states.shape[-1]
    wide = query_states.shape[-1]
    shape = jax.ShapeDtypeStruct
    flat = (row_count, wide)
    small = (row_count, width)
    length = shards // PAIR
    dma = pltpu.SemaphoreType.DMA
    def pinned(array):
        return pltpu.with_memory_space_constraint(array, pltpu.HBM)

    hbm = pl.BlockSpec(memory_space=pltpu.HBM)
    shapes = tuple(shape(dims, jnp.bfloat16) for dims in (flat, flat, small, small))
    results = pl.pallas_call(
        local_kernel,
        out_shape=shapes,
        in_specs=[pl.BlockSpec(memory_space=pltpu.SMEM)] + [hbm] * 4,
        out_specs=[pl.BlockSpec(memory_space=pltpu.VMEM)] * 4,
        scratch_shapes=[
            pltpu.VMEM((shards, 8, 128), jnp.int32),
            pltpu.VMEM((bands, shards, 2, rows, width), jnp.bfloat16),
            pltpu.VMEM(flat, jnp.bfloat16),
            pltpu.VMEM(flat, jnp.bfloat16),
            pltpu.VMEM((bands, shards, 2, rows, width), jnp.float32),
        ]
        + [pltpu.VMEM((bands, length, 2, rows, width), jnp.bfloat16)] * 4
        + [
            dma((4,)),
            dma((shards,)),
            dma((shards,)),
            dma((2 * bands * shards,)),
            dma((bands, shards)),
        ]
        + [dma((bands, length))] * 4,
        compiler_params=pltpu.CompilerParams(
            collective_id=0, has_side_effects=True, vmem_limit_bytes=48 << 20
        ),
    )(
        doc_lengths,
        pinned(query_states.reshape(flat)),
        pinned(key_states.reshape(bands, rows, width)),
        pinned(value_state_array.reshape(bands, rows, width)),
        pinned(grad_output.reshape(flat)),
    )
    results = pl.pallas_call(
        hand_over,
        out_shape=shapes,
        in_specs=[pl.BlockSpec(memory_space=pl.ANY)] * 4,
        out_specs=[hbm] * 4,
        scratch_shapes=[dma((4,))],
        compiler_params=pltpu.CompilerParams(vmem_limit_bytes=1 << 20),
    )(*results)
    return tuple(result[:, None, :] for result in results)


def solution(mesh):
    in_specs = (
        P(None, "dp", "mp"),
        P(None, "dp", "mp"),
        P(None, "dp", "mp"),
        P(None, "dp", "mp"),
        P("dp"),
    )
    out_specs = (P(None, "dp", "mp"), P(None, "dp", "mp"), P(None, "dp", "mp"), P(None, "dp", "mp"))
    return jax.shard_map(
        per_device, mesh=mesh, in_specs=in_specs, out_specs=out_specs, check_vma=False
    )
```

```python
import jax
import jax.numpy as jnp
from jax import lax
from jax.experimental import pallas as pl
from jax.experimental.pallas import tpu as pltpu
from jax.sharding import PartitionSpec as P

QUERY_HEADS = 64
KEY_VALUE_HEADS = 8
HEAD_SIZE = 128


def contract(form, first, second):
    return jnp.einsum(form, first, second, preferred_element_type=jnp.float32)


def forward_tile(query_rows, key_row_block, value_row_block, length, first_row):
    scaling = query_rows.shape[-1] ** (-0.5)
    row_place = first_row + jnp.arange(query_rows.shape[0], dtype=jnp.int32)
    key_place = jnp.arange(key_row_block.shape[0], dtype=jnp.int32)
    allowed = (key_place[None, :] <= row_place[:, None]) & (key_place[None, :] < length)
    scores = contract("qhge,khe->hgqk", query_rows, key_row_block) * scaling
    scores = jnp.where(allowed, scores, -1e30)
    row_max = jnp.max(scores, axis=-1, keepdims=True)
    raised = jnp.exp(scores - row_max)
    attn_weights = raised / jnp.sum(raised, axis=-1, keepdims=True)
    attn_weights = jnp.where((row_place < length)[:, None], attn_weights, 0.0)
    rounded = attn_weights.astype(jnp.bfloat16)
    attended = contract("hgqk,khe->qhge", rounded, value_row_block).astype(jnp.bfloat16)
    return (attended, attn_weights, rounded)


def backward_tile(
    query_rows, key_row_block, value_row_block, gradient_row_block, attended, attn_weights, rounded
):
    scaling = query_rows.shape[-1] ** (-0.5)
    dprobs = contract("qhge,khe->hgqk", gradient_row_block, value_row_block)
    row_dot = jnp.sum(
        gradient_row_block.astype(jnp.float32) * attended.astype(jnp.float32), axis=-1
    )
    row_dot = jnp.transpose(row_dot, (1, 2, 0))[..., None]
    dscores = (attn_weights * (dprobs - row_dot)).astype(jnp.bfloat16)
    dquery = (contract("hgqk,khe->qhge", dscores, key_row_block) * scaling).astype(jnp.bfloat16)
    key_total = contract("hgqk,qhge->khe", dscores, query_rows) * scaling
    value_total = contract("hgqk,qhge->khe", rounded, gradient_row_block)
    return (dquery, key_total, value_total)


def per_device_by_document(query_states, key_states, value_state_array, grad_output, doc_lengths):
    shards = lax.axis_size("dp")
    source = lax.axis_index("dp")
    lengths = lax.all_gather(doc_lengths, "dp", axis=0, tiled=True)
    owners = jnp.arange(shards, dtype=jnp.int32)
    starts = jnp.sum(jnp.where(owners[None, :] < owners[:, None], lengths[None, :], 0), axis=1)
    row_count = query_states.shape[0]
    slot_capacity = 2 * row_count
    per_peer = slot_capacity // shards
    kv_heads = key_states.shape[-1] // HEAD_SIZE
    query_group = QUERY_HEADS // KEY_VALUE_HEADS
    places = jnp.arange(per_peer, dtype=jnp.int32)
    offsets = jnp.mod(source - starts, shards)
    within = places[:, None] * shards + offsets[None, :]
    sendable = within < lengths[None, :]
    local_rows = jnp.where(sendable, (starts[None, :] + within - source) // shards, -1)
    my_start = jnp.sum(jnp.where(owners == source, starts, 0))
    my_length = jnp.sum(jnp.where(owners == source, lengths, 0))
    token_ids = jnp.arange(row_count, dtype=jnp.int32) * shards + source
    begun = starts[None, :] <= token_ids[:, None]
    owner_index = jnp.sum(begun.astype(jnp.int32), axis=1) - 1
    home_slot = token_ids - jnp.max(jnp.where(begun, starts[None, :], 0), axis=1)
    home_index = home_slot // shards * shards + owner_index

    def pick(index, flat):
        chosen = index[:, None] == jnp.arange(flat.shape[0], dtype=jnp.int32)[None, :]
        return contract("ij,jk->ik", chosen.astype(flat.dtype), flat).astype(flat.dtype)

    def pack_rows(states):
        flat = states[:, 0, :]
        return pick(local_rows.reshape(-1), flat).reshape(per_peer, shards, flat.shape[-1])

    def arrive(received):
        rolled = jnp.roll(received, -my_start, axis=1)
        return rolled.reshape(slot_capacity, received.shape[-1])

    def as_queries(flat):
        return flat.reshape(slot_capacity, kv_heads, query_group, HEAD_SIZE)

    def as_keys(flat):
        return flat.reshape(slot_capacity, kv_heads, HEAD_SIZE)

    def depart(slots):
        return jnp.roll(slots.reshape(per_peer, shards, -1), my_start, axis=1)

    def settle(received):
        flat = received.reshape(slot_capacity, received.shape[-1])
        return pick(home_index, flat)[:, None, :]

    spans = [(0, slot_capacity, slot_capacity)]
    arrived = (
        lax.all_to_all(pack_rows(query_states), "dp", split_axis=1, concat_axis=1, tiled=True),
        lax.all_to_all(pack_rows(key_states), "dp", split_axis=1, concat_axis=1, tiled=True),
        lax.all_to_all(pack_rows(value_state_array), "dp", split_axis=1, concat_axis=1, tiled=True),
    )
    query_rows = as_queries(arrive(arrived[0]))
    key_row_block = as_keys(arrive(arrived[1]))
    value_row_block = as_keys(arrive(arrived[2]))
    first_row, row_span, key_reach = spans[0]

    def compute(first_row=first_row, row_span=row_span, key_reach=key_reach):
        return forward_tile(query_rows, key_row_block, value_row_block, my_length, first_row)

    pieces = [compute()]
    attended = jnp.concatenate([piece[0] for piece in pieces], axis=0)
    output_home = lax.all_to_all(depart(attended), "dp", split_axis=1, concat_axis=1, tiled=True)
    grad_arrived = lax.all_to_all(
        pack_rows(grad_output), "dp", split_axis=1, concat_axis=1, tiled=True
    )
    gradient_row_block = as_queries(arrive(grad_arrived))
    query_parts = []
    key_total = jnp.zeros((slot_capacity, kv_heads, HEAD_SIZE), jnp.float32)
    value_total = jnp.zeros((slot_capacity, kv_heads, HEAD_SIZE), jnp.float32)
    for (first_row, row_span, key_reach), piece in zip(spans, pieces):

        def compute(first_row=first_row, row_span=row_span, key_reach=key_reach, piece=piece):
            return backward_tile(
                query_rows,
                key_row_block,
                value_row_block,
                gradient_row_block,
                piece[0],
                piece[1],
                piece[2],
            )

        result = compute()
        query_parts.append(result[0])
        key_total = key_total.at[:key_reach].add(result[1])
        value_total = value_total.at[:key_reach].add(result[2])
    dquery = query_parts[0]
    dquery, key_part, value_part = (
        dquery,
        key_total.astype(jnp.bfloat16),
        value_total.astype(jnp.bfloat16),
    )
    returned = (
        lax.all_to_all(depart(dquery), "dp", split_axis=1, concat_axis=1, tiled=True),
        lax.all_to_all(depart(key_part), "dp", split_axis=1, concat_axis=1, tiled=True),
        lax.all_to_all(depart(value_part), "dp", split_axis=1, concat_axis=1, tiled=True),
    )
    return (settle(output_home), settle(returned[0]), settle(returned[1]), settle(returned[2]))


MESH = pl.DeviceIdType.MESH
LOG2E = 1.4426950408889634
SPAN = 256
PAIR = 2
LINE = 4
STEPS = (
    (
        "s0004", "s2001", "s1004", "s0002", "s1002", "s3001", "s3004", "s0001", "s1011", "s0011", "s1104", "s1204",
        "s1001", "s3011", "s2004", "s0104", "s0204", "s0304", "s2304", "s3204", "c00", "s3304", "c01", "c10",
        "c11", "p02", "p03", "p01", "c20", "c21", "p13", "p11", "p12", "c30", "l02", "c31",
        "l03", "p33", "p32", "p23", "l13", "p22", "l11", "p31", "p00", "l12", "l33", "p21",
        "l32", "p30", "l01", "p20", "p10", "l23", "l31", "l22", "e0", "l21", "e3", "e2",
        "e1",
    ),
    (
        "s0102", "s2104", "s1103", "s1100", "s3104", "s0100", "s0104", "s0204", "s1102", "s0200", "s1104", "s2110",
        "s2002", "s2102", "s2112", "s0304", "s3103", "s0300", "s1304", "s3110", "s1300", "s1204", "s3003", "s2300",
        "s2304", "s2004", "s3112", "c00", "s1310", "s2210", "s3102", "s2200", "s2100", "s3002", "s3100", "c01",
        "s3012", "c10", "c11", "p02", "c20", "p03", "c21", "p12", "p13", "c30", "p00", "l02",
        "c31", "l03", "p23", "p33", "p22", "p01", "l12", "p30", "l13", "p32", "p20", "l00",
        "p10", "l23", "p11", "p31", "l33", "l30", "l22", "l20", "l10", "e1", "l32", "p21",
        "e3", "e0", "e2",
    ),
)

def attend(refs, me, band, head, mask, group):
    kv, q_buf, g_buf, attn_ref, dq_ref, total = refs
    shards, rows = kv.shape[1], kv.shape[3]
    first = max(band - 1, 0)
    keys = (band - first + 1) * shards * rows
    scale = HEAD_SIZE**-0.5
    lanes = pl.ds(head * HEAD_SIZE, HEAD_SIZE)
    here = pl.ds(band * rows, rows)

    def stack(buf):
        base = head * group
        return jnp.concatenate(
            [buf[here, pl.ds((base + g) * HEAD_SIZE, HEAD_SIZE)] for g in range(group)], axis=0
        )

    def dot(first_one, second_one, dims):
        return lax.dot_general(
            first_one, second_one, (dims, ((), ())), preferred_element_type=jnp.float32
        )

    key_rows = kv[first : band + 1, :, 0, :, lanes].reshape(keys, HEAD_SIZE)
    value_rows = kv[first : band + 1, :, 1, :, lanes].reshape(keys, HEAD_SIZE)
    query = stack(q_buf)
    grad = stack(g_buf)
    scores = jnp.where(mask, dot(key_rows, query, ((1,), (1,))), -1e30)
    dprobs = dot(value_rows, grad, ((1,), (1,)))
    top = jnp.max(scores, axis=0, keepdims=True)
    raised = jnp.exp2((scores - top) * (scale * LOG2E))
    probs = raised * (1.0 / jnp.sum(raised, axis=0, keepdims=True))
    low = probs.astype(jnp.bfloat16)
    weighted = probs * dprobs
    delta = jnp.sum(weighted, axis=0, keepdims=True)
    dscores = (weighted - probs * delta).astype(jnp.bfloat16)
    attended = dot(value_rows, low, ((0,), (0,))).T.astype(jnp.bfloat16)
    dquery = (dot(key_rows, dscores, ((0,), (0,))) * scale).T.astype(jnp.bfloat16)
    for g in range(group):
        columns = pl.ds((head * group + g) * HEAD_SIZE, HEAD_SIZE)
        attn_ref[here, columns] = attended[g * rows : (g + 1) * rows]
        dq_ref[here, columns] = dquery[g * rows : (g + 1) * rows]
    parts = (dot(dscores, query, ((1,), (0,))), dot(low, grad, ((1,), (0,))))
    size = shards * rows
    for kind, part in enumerate(parts):
        if first < band:
            total[first, :, kind, :, lanes] += part[:size].reshape(shards, rows, HEAD_SIZE)
        total[band, :, kind, :, lanes] = part[keys - size :].reshape(shards, rows, HEAD_SIZE)


def local_kernel(
    len_ref, q_hbm, k_hbm, v_hbm, g_hbm, attn_ref, dq_ref, dk_ref, dv_ref,
    lens, kv, q_buf, g_buf, total, pair_out, pair_in, line_out, line_in,
    local_sem, len_send, len_recv, kv_send, kv_recv,
    pair_sum_send, pair_sum_recv, line_sum_send, line_sum_recv,
):
    me = lax.axis_index("dp")
    bands, shards, _, rows, width = kv.shape
    heads = width // HEAD_SIZE
    group = q_buf.shape[1] // width
    length = shards // PAIR
    y = lax.rem(me, PAIR)
    z = lax.div(me, PAIR)
    slot = y * length + z
    partner = z * PAIR + 1 - y
    peers = [lax.rem(me + o, shards) for o in range(1, shards)]

    def push(src, dst, send, recv, peer):
        return pltpu.make_async_remote_copy(
            src_ref=src, dst_ref=dst, send_sem=send, recv_sem=recv,
            device_id={"dp": peer}, device_id_type=MESH,
        )

    loads = [
        pltpu.make_async_copy(k_hbm, kv.at[:, slot, 0], local_sem.at[0]),
        pltpu.make_async_copy(v_hbm, kv.at[:, slot, 1], local_sem.at[1]),
        pltpu.make_async_copy(q_hbm, q_buf, local_sem.at[2]),
        pltpu.make_async_copy(g_hbm, g_buf, local_sem.at[3]),
    ]
    for load in loads:
        load.start()
    barrier = pltpu.get_barrier_semaphore()
    for peer in peers:
        pl.semaphore_signal(barrier, inc=1, device_id={"dp": peer}, device_id_type=MESH)
    lens[me] = jnp.full(lens.shape[1:], len_ref[0], jnp.int32)
    pl.semaphore_wait(barrier, shards - 1)
    sends = []
    moves = [[] for _ in range(length)]
    known = [set() for _ in range(length)]

    def go(copy):
        copy.start()
        sends.append(copy)

    def edge(k):
        return k in (0, length - 1)

    def there(rel, s):
        return (y if rel == 0 else 1 - y) * length + s

    def piece(band, rel, s):
        return kv.at[band, there(rel, s)]

    def sending(at, band, rel, s, target):
        over = target == length
        return push(
            piece(band, rel, s), piece(band, rel, s), kv_send.at[at],
            kv_recv.at[band, (1 - rel if over else rel) * length + s],
            partner if over else target * PAIR + y,
        )

    def arrived(k, band, rel, s):
        if (rel, s) != (0, k) and (band, rel, s) not in known[k]:
            known[k].add((band, rel, s))
            push(
                piece(band, rel, s), piece(band, rel, s), kv_send.at[0],
                kv_recv.at[band, rel * length + s], partner,
            ).wait_recv()

    def each(body):
        for k in range(length):
            pl.when(z == k)(lambda k=k: body(k))

    def across(band, s):
        return push(
            pair_out.at[band, s], pair_in.at[band, s],
            pair_sum_send.at[band, s], pair_sum_recv.at[band, s], partner,
        )

    def along(band, source, target):
        return push(
            line_out.at[band, target], line_in.at[band, source],
            line_sum_send.at[band, target], line_sum_recv.at[band, source], target * PAIR + y,
        )

    def relay(k, band, s, rel, target):
        arrived(k, band, rel, s)
        sending(len(moves[k]), band, rel, s, target).start()
        moves[k].append((band, rel, s, target))

    def pair_sum(k, band, s):
        pair_out[band, s] = total[band, there(1, s)].astype(jnp.bfloat16)
        across(band, s).start()

    def line_sum(k, band, s):
        across(band, s).wait_recv()
        both = total[band, there(0, s)] + pair_in[band, s].astype(jnp.float32)
        line_out[band, s] = both.astype(jnp.bfloat16)
        along(band, k, s).start()

    def drain(k):
        for at, which in enumerate(moves[k]):
            sending(at, *which).wait_send()
        for band in range(bands):
            for s in range(length):
                across(band, s).wait_send()
                if s != k:
                    along(band, k, s).wait_send()

    def finish(k, band):
        across(band, k).wait_recv()
        sums = total[band, there(0, k)] + pair_in[band, k].astype(jnp.float32)
        for s in range(length):
            if s == k:
                continue
            along(band, s, k).wait_recv()
            sums = sums + line_in[band, s].astype(jnp.float32)
        here = pl.ds(band * rows, rows)
        dk_ref[here, :] = (sums[0] * HEAD_SIZE**-0.5).astype(jnp.bfloat16)
        dv_ref[here, :] = sums[1].astype(jnp.bfloat16)

    for at, peer in enumerate(peers):
        go(push(lens.at[me], lens.at[me], len_send.at[at], len_recv.at[me], peer))
    loads[0].wait()
    loads[1].wait()
    columns = group * rows
    lane_row = lax.rem(lax.broadcasted_iota(jnp.int32, (1, columns), 1), rows)
    starts = []

    def documents():
        for at, peer in enumerate(peers):
            push(
                lens.at[peer], lens.at[peer], len_send.at[at], len_recv.at[peer], peer
            ).wait_recv()
        running = jnp.zeros((1, lens.shape[-1]), jnp.int32)
        for b in range(shards):
            starts.append(jnp.concatenate([running] * (columns // lens.shape[-1]), axis=1))
            running = running + lens[b, 0:1, :]
        loads[2].wait()
        loads[3].wait()

    def compute(band, head):
        first = max(band - 1, 0)
        if head == 0:
            token = (band * rows + lane_row) * shards + me
            begin_at = jnp.zeros_like(token)
            for s in starts:
                begin_at = jnp.where(s <= token, s, begin_at)
            block = (band - first + 1, PAIR, length, rows, columns)
            iota = [lax.broadcasted_iota(jnp.int32, block, axis) for axis in range(4)]
            key_row = (first + iota[0]) * rows + iota[3]
            key_token = (key_row * shards + iota[2] * PAIR + iota[1]).reshape(-1, columns)
            masks[band] = (key_token <= token) & (key_token >= begin_at)
            each(lambda k: [arrived(k, band, rel, s) for rel in (0, 1) for s in range(length)] and None)
        attend((kv, q_buf, g_buf, attn_ref, dq_ref, total), me, band, head, masks[band], group)

    def act(k, step):
        kind, band, *which = step[0], *(int(digit) for digit in step[1:])
        flip = (lambda at: length - 1 - at) if k >= length // 2 else (lambda at: at)
        if kind == "s":
            s, rel, target = which
            relay(k, band, flip(s), rel, target if target == length else flip(target))
        elif kind == "p":
            pair_sum(k, band, flip(which[0]))
        elif kind == "l":
            line_sum(k, band, flip(which[0]))
        else:
            finish(k, band)

    masks = {}
    queues = [list(STEPS[0 if edge(k) else 1]) for k in range(length)]

    def pump(k):
        while queues[k] and queues[k][0][0] != "c":
            act(k, queues[k].pop(0))

    def begin(k):
        while queues[k][0][0] == "s" and queues[k][0][2:4] == ("00" if edge(k) else "10"):
            act(k, queues[k].pop(0))

    each(begin)
    while True:
        each(pump)
        if not queues[0]:
            break
        if not starts:
            documents()
        step = queues[0][0]
        for queue in queues:
            queue.pop(0)
        compute(int(step[1]), int(step[2]))
    for send in sends:
        send.wait_send()
    each(drain)


def hand_over(*refs):
    count = len(refs) // 2
    sems = refs[-1]
    copies = [
        pltpu.make_async_copy(refs[at], refs[count + at], sems.at[at]) for at in range(count)
    ]
    for copy in copies:
        copy.start()
    for copy in copies:
        copy.wait()


def per_device(query_states, key_states, value_state_array, grad_output, doc_lengths):
    shards = lax.axis_size("dp")
    row_count = query_states.shape[0]
    rows = SPAN // shards
    if rows % 16 or row_count % rows or shards != PAIR * LINE:
        return per_device_by_document(
            query_states, key_states, value_state_array, grad_output, doc_lengths
        )
    bands = row_count // rows
    width = key_states.shape[-1]
    wide = query_states.shape[-1]
    shape = jax.ShapeDtypeStruct
    flat = (row_count, wide)
    small = (row_count, width)
    length = shards // PAIR
    dma = pltpu.SemaphoreType.DMA
    def pinned(array):
        return pltpu.with_memory_space_constraint(array, pltpu.HBM)

    hbm = pl.BlockSpec(memory_space=pltpu.HBM)
    shapes = tuple(shape(dims, jnp.bfloat16) for dims in (flat, flat, small, small))
    results = pl.pallas_call(
        local_kernel,
        out_shape=shapes,
        in_specs=[pl.BlockSpec(memory_space=pltpu.SMEM)] + [hbm] * 4,
        out_specs=[pl.BlockSpec(memory_space=pltpu.VMEM)] * 4,
        scratch_shapes=[
            pltpu.VMEM((shards, 1, 128), jnp.int32),
            pltpu.VMEM((bands, shards, 2, rows, width), jnp.bfloat16),
            pltpu.VMEM(flat, jnp.bfloat16),
            pltpu.VMEM(flat, jnp.bfloat16),
            pltpu.VMEM((bands, shards, 2, rows, width), jnp.float32),
        ]
        + [pltpu.VMEM((bands, length, 2, rows, width), jnp.bfloat16)] * 4
        + [
            dma((4,)),
            dma((shards,)),
            dma((shards,)),
            dma((2 * bands * shards,)),
            dma((bands, shards)),
        ]
        + [dma((bands, length))] * 4,
        compiler_params=pltpu.CompilerParams(
            collective_id=0, has_side_effects=True, vmem_limit_bytes=48 << 20
        ),
    )(
        doc_lengths,
        pinned(query_states.reshape(flat)),
        pinned(key_states.reshape(bands, rows, width)),
        pinned(value_state_array.reshape(bands, rows, width)),
        pinned(grad_output.reshape(flat)),
    )
    results = pl.pallas_call(
        hand_over,
        out_shape=shapes,
        in_specs=[pl.BlockSpec(memory_space=pl.ANY)] * 4,
        out_specs=[hbm] * 4,
        scratch_shapes=[dma((4,))],
        compiler_params=pltpu.CompilerParams(vmem_limit_bytes=1 << 20),
    )(*results)
    return tuple(result[:, None, :] for result in results)


def solution(mesh):
    in_specs = (
        P(None, "dp", "mp"),
        P(None, "dp", "mp"),
        P(None, "dp", "mp"),
        P(None, "dp", "mp"),
        P("dp"),
    )
    out_specs = (P(None, "dp", "mp"), P(None, "dp", "mp"), P(None, "dp", "mp"), P(None, "dp", "mp"))
    return jax.shard_map(
        per_device, mesh=mesh, in_specs=in_specs, out_specs=out_specs, check_vma=False
    )
```

```python
import jax
import jax.numpy as jnp
from jax import lax
from jax.experimental import pallas as pl
from jax.experimental.pallas import tpu as pltpu
from jax.sharding import PartitionSpec as P

QUERY_HEADS = 64
KEY_VALUE_HEADS = 8
HEAD_SIZE = 128


def contract(form, first, second):
    return jnp.einsum(form, first, second, preferred_element_type=jnp.float32)


def forward_tile(query_rows, key_row_block, value_row_block, length, first_row):
    scaling = query_rows.shape[-1] ** (-0.5)
    row_place = first_row + jnp.arange(query_rows.shape[0], dtype=jnp.int32)
    key_place = jnp.arange(key_row_block.shape[0], dtype=jnp.int32)
    allowed = (key_place[None, :] <= row_place[:, None]) & (key_place[None, :] < length)
    scores = contract("qhge,khe->hgqk", query_rows, key_row_block) * scaling
    scores = jnp.where(allowed, scores, -1e30)
    row_max = jnp.max(scores, axis=-1, keepdims=True)
    raised = jnp.exp(scores - row_max)
    attn_weights = raised / jnp.sum(raised, axis=-1, keepdims=True)
    attn_weights = jnp.where((row_place < length)[:, None], attn_weights, 0.0)
    rounded = attn_weights.astype(jnp.bfloat16)
    attended = contract("hgqk,khe->qhge", rounded, value_row_block).astype(jnp.bfloat16)
    return (attended, attn_weights, rounded)


def backward_tile(
    query_rows, key_row_block, value_row_block, gradient_row_block, attended, attn_weights, rounded
):
    scaling = query_rows.shape[-1] ** (-0.5)
    dprobs = contract("qhge,khe->hgqk", gradient_row_block, value_row_block)
    row_dot = jnp.sum(
        gradient_row_block.astype(jnp.float32) * attended.astype(jnp.float32), axis=-1
    )
    row_dot = jnp.transpose(row_dot, (1, 2, 0))[..., None]
    dscores = (attn_weights * (dprobs - row_dot)).astype(jnp.bfloat16)
    dquery = (contract("hgqk,khe->qhge", dscores, key_row_block) * scaling).astype(jnp.bfloat16)
    key_total = contract("hgqk,qhge->khe", dscores, query_rows) * scaling
    value_total = contract("hgqk,qhge->khe", rounded, gradient_row_block)
    return (dquery, key_total, value_total)


def per_device_by_document(query_states, key_states, value_state_array, grad_output, doc_lengths):
    shards = lax.axis_size("dp")
    source = lax.axis_index("dp")
    lengths = lax.all_gather(doc_lengths, "dp", axis=0, tiled=True)
    owners = jnp.arange(shards, dtype=jnp.int32)
    starts = jnp.sum(jnp.where(owners[None, :] < owners[:, None], lengths[None, :], 0), axis=1)
    row_count = query_states.shape[0]
    slot_capacity = 2 * row_count
    per_peer = slot_capacity // shards
    kv_heads = key_states.shape[-1] // HEAD_SIZE
    query_group = QUERY_HEADS // KEY_VALUE_HEADS
    places = jnp.arange(per_peer, dtype=jnp.int32)
    offsets = jnp.mod(source - starts, shards)
    within = places[:, None] * shards + offsets[None, :]
    sendable = within < lengths[None, :]
    local_rows = jnp.where(sendable, (starts[None, :] + within - source) // shards, -1)
    my_start = jnp.sum(jnp.where(owners == source, starts, 0))
    my_length = jnp.sum(jnp.where(owners == source, lengths, 0))
    token_ids = jnp.arange(row_count, dtype=jnp.int32) * shards + source
    begun = starts[None, :] <= token_ids[:, None]
    owner_index = jnp.sum(begun.astype(jnp.int32), axis=1) - 1
    home_slot = token_ids - jnp.max(jnp.where(begun, starts[None, :], 0), axis=1)
    home_index = home_slot // shards * shards + owner_index

    def pick(index, flat):
        chosen = index[:, None] == jnp.arange(flat.shape[0], dtype=jnp.int32)[None, :]
        return contract("ij,jk->ik", chosen.astype(flat.dtype), flat).astype(flat.dtype)

    def pack_rows(states):
        flat = states[:, 0, :]
        return pick(local_rows.reshape(-1), flat).reshape(per_peer, shards, flat.shape[-1])

    def arrive(received):
        rolled = jnp.roll(received, -my_start, axis=1)
        return rolled.reshape(slot_capacity, received.shape[-1])

    def as_queries(flat):
        return flat.reshape(slot_capacity, kv_heads, query_group, HEAD_SIZE)

    def as_keys(flat):
        return flat.reshape(slot_capacity, kv_heads, HEAD_SIZE)

    def depart(slots):
        return jnp.roll(slots.reshape(per_peer, shards, -1), my_start, axis=1)

    def settle(received):
        flat = received.reshape(slot_capacity, received.shape[-1])
        return pick(home_index, flat)[:, None, :]

    spans = [(0, slot_capacity, slot_capacity)]
    arrived = (
        lax.all_to_all(pack_rows(query_states), "dp", split_axis=1, concat_axis=1, tiled=True),
        lax.all_to_all(pack_rows(key_states), "dp", split_axis=1, concat_axis=1, tiled=True),
        lax.all_to_all(pack_rows(value_state_array), "dp", split_axis=1, concat_axis=1, tiled=True),
    )
    query_rows = as_queries(arrive(arrived[0]))
    key_row_block = as_keys(arrive(arrived[1]))
    value_row_block = as_keys(arrive(arrived[2]))
    first_row, row_span, key_reach = spans[0]

    def compute(first_row=first_row, row_span=row_span, key_reach=key_reach):
        return forward_tile(query_rows, key_row_block, value_row_block, my_length, first_row)

    pieces = [compute()]
    attended = jnp.concatenate([piece[0] for piece in pieces], axis=0)
    output_home = lax.all_to_all(depart(attended), "dp", split_axis=1, concat_axis=1, tiled=True)
    grad_arrived = lax.all_to_all(
        pack_rows(grad_output), "dp", split_axis=1, concat_axis=1, tiled=True
    )
    gradient_row_block = as_queries(arrive(grad_arrived))
    query_parts = []
    key_total = jnp.zeros((slot_capacity, kv_heads, HEAD_SIZE), jnp.float32)
    value_total = jnp.zeros((slot_capacity, kv_heads, HEAD_SIZE), jnp.float32)
    for (first_row, row_span, key_reach), piece in zip(spans, pieces):

        def compute(first_row=first_row, row_span=row_span, key_reach=key_reach, piece=piece):
            return backward_tile(
                query_rows,
                key_row_block,
                value_row_block,
                gradient_row_block,
                piece[0],
                piece[1],
                piece[2],
            )

        result = compute()
        query_parts.append(result[0])
        key_total = key_total.at[:key_reach].add(result[1])
        value_total = value_total.at[:key_reach].add(result[2])
    dquery = query_parts[0]
    dquery, key_part, value_part = (
        dquery,
        key_total.astype(jnp.bfloat16),
        value_total.astype(jnp.bfloat16),
    )
    returned = (
        lax.all_to_all(depart(dquery), "dp", split_axis=1, concat_axis=1, tiled=True),
        lax.all_to_all(depart(key_part), "dp", split_axis=1, concat_axis=1, tiled=True),
        lax.all_to_all(depart(value_part), "dp", split_axis=1, concat_axis=1, tiled=True),
    )
    return (settle(output_home), settle(returned[0]), settle(returned[1]), settle(returned[2]))


MESH = pl.DeviceIdType.MESH
LOG2E = 1.4426950408889634
SPAN = 256
PAIR = 2
LINE = 4
STEPS = (
    (
        "s0004", "s2001", "s1004", "s0002", "s1002", "s3001", "s3004", "s0001", "s1011", "s0011", "s1104", "s1204",
        "s1001", "s3011", "s2004", "s0104", "s0204", "s0304", "s2304", "s3204", "c00", "s3304", "c01", "c10",
        "c11", "p02", "p03", "p01", "c20", "c21", "p13", "p11", "p12", "c30", "l02", "c31",
        "l03", "p33", "p32", "p23", "l13", "p22", "l11", "p31", "p00", "l12", "l33", "p21",
        "l32", "p30", "l01", "p20", "p10", "l23", "l31", "l22", "e0", "l21", "e3", "e2",
        "e1",
    ),
    (
        "s0102", "s2104", "s1103", "s1100", "s3104", "s0100", "s0104", "s0204", "s1102", "s0200", "s1104", "s2110",
        "s2002", "s2102", "s2112", "s0304", "s3103", "s0300", "s1304", "s3110", "s1300", "s1204", "s3003", "s2300",
        "s2304", "s2004", "s3112", "c00", "s1310", "s2210", "s3102", "s2200", "s2100", "s3002", "s3100", "c01",
        "s3012", "c10", "c11", "p02", "c20", "p03", "c21", "p12", "p13", "c30", "p00", "l02",
        "c31", "l03", "p23", "p33", "p22", "p01", "l12", "p30", "l13", "p32", "p20", "l00",
        "p10", "l23", "p11", "p31", "l33", "l30", "l22", "l20", "l10", "e1", "l32", "p21",
        "e3", "e0", "e2",
    ),
)

def attend(refs, me, band, head, mask, group):
    kv, q_buf, g_buf, attn_ref, dq_ref, total = refs
    shards, rows = kv.shape[1], kv.shape[3]
    first = max(band - 1, 0)
    keys = (band - first + 1) * shards * rows
    scale = HEAD_SIZE**-0.5
    lanes = pl.ds(head * HEAD_SIZE, HEAD_SIZE)
    here = pl.ds(band * rows, rows)

    def stack(buf):
        base = head * group
        return jnp.concatenate(
            [buf[here, pl.ds((base + g) * HEAD_SIZE, HEAD_SIZE)] for g in range(group)], axis=0
        )

    def dot(first_one, second_one, dims):
        return lax.dot_general(
            first_one, second_one, (dims, ((), ())), preferred_element_type=jnp.float32
        )

    key_rows = kv[first : band + 1, :, 0, :, lanes].reshape(keys, HEAD_SIZE)
    value_rows = kv[first : band + 1, :, 1, :, lanes].reshape(keys, HEAD_SIZE)
    query = stack(q_buf)
    grad = stack(g_buf)
    scores = jnp.where(mask, dot(key_rows, query, ((1,), (1,))), -1e30)
    dprobs = dot(value_rows, grad, ((1,), (1,)))
    top = jnp.max(scores, axis=0, keepdims=True)
    raised = jnp.exp2((scores - top) * (scale * LOG2E))
    probs = raised * (1.0 / jnp.sum(raised, axis=0, keepdims=True))
    low = probs.astype(jnp.bfloat16)
    weighted = probs * dprobs
    delta = jnp.sum(weighted, axis=0, keepdims=True)
    dscores = (weighted - probs * delta).astype(jnp.bfloat16)
    attended = dot(value_rows, low, ((0,), (0,))).T.astype(jnp.bfloat16)
    dquery = (dot(key_rows, dscores, ((0,), (0,))) * scale).T.astype(jnp.bfloat16)
    for g in range(group):
        columns = pl.ds((head * group + g) * HEAD_SIZE, HEAD_SIZE)
        attn_ref[here, columns] = attended[g * rows : (g + 1) * rows]
        dq_ref[here, columns] = dquery[g * rows : (g + 1) * rows]
    parts = (dot(dscores, query, ((1,), (0,))), dot(low, grad, ((1,), (0,))))
    size = shards * rows
    for kind, part in enumerate(parts):
        if first < band:
            total[first, :, kind, :, lanes] += part[:size].reshape(shards, rows, HEAD_SIZE)
        total[band, :, kind, :, lanes] = part[keys - size :].reshape(shards, rows, HEAD_SIZE)


def local_kernel(
    len_ref, q_hbm, k_hbm, v_hbm, g_hbm, attn_ref, dq_ref, dk_ref, dv_ref,
    lens, kv, q_buf, g_buf, total, pair_out, pair_in, line_out, line_in,
    local_sem, len_send, len_recv, kv_send, kv_recv,
    pair_sum_send, pair_sum_recv, line_sum_send, line_sum_recv,
):
    me = lax.axis_index("dp")
    bands, shards, _, rows, width = kv.shape
    heads = width // HEAD_SIZE
    group = q_buf.shape[1] // width
    length = shards // PAIR
    y = lax.rem(me, PAIR)
    z = lax.div(me, PAIR)
    slot = y * length + z
    partner = z * PAIR + 1 - y
    peers = [lax.rem(me + o, shards) for o in range(1, shards)]

    def push(src, dst, send, recv, peer):
        return pltpu.make_async_remote_copy(
            src_ref=src, dst_ref=dst, send_sem=send, recv_sem=recv,
            device_id={"dp": peer}, device_id_type=MESH,
        )

    loads = [
        pltpu.make_async_copy(k_hbm, kv.at[:, slot, 0], local_sem.at[0]),
        pltpu.make_async_copy(v_hbm, kv.at[:, slot, 1], local_sem.at[1]),
        pltpu.make_async_copy(q_hbm, q_buf, local_sem.at[2]),
        pltpu.make_async_copy(g_hbm, g_buf, local_sem.at[3]),
    ]
    barrier = pltpu.get_barrier_semaphore()
    for peer in peers:
        pl.semaphore_signal(barrier, inc=1, device_id={"dp": peer}, device_id_type=MESH)
    for load in loads:
        load.start()
    lens[me] = jnp.full(lens.shape[1:], len_ref[0], jnp.int32)
    pl.semaphore_wait(barrier, shards - 1)
    sends = []
    moves = [[] for _ in range(length)]
    known = [set() for _ in range(length)]

    def go(copy):
        copy.start()
        sends.append(copy)

    def edge(k):
        return k in (0, length - 1)

    def there(rel, s):
        return (y if rel == 0 else 1 - y) * length + s

    def piece(band, rel, s):
        return kv.at[band, there(rel, s)]

    def sending(at, band, rel, s, target):
        over = target == length
        return push(
            piece(band, rel, s), piece(band, rel, s), kv_send.at[at],
            kv_recv.at[band, (1 - rel if over else rel) * length + s],
            partner if over else target * PAIR + y,
        )

    def arrived(k, band, rel, s):
        if (rel, s) != (0, k) and (band, rel, s) not in known[k]:
            known[k].add((band, rel, s))
            push(
                piece(band, rel, s), piece(band, rel, s), kv_send.at[0],
                kv_recv.at[band, rel * length + s], partner,
            ).wait_recv()

    def each(body):
        for k in range(length):
            pl.when(z == k)(lambda k=k: body(k))

    def across(band, s):
        return push(
            pair_out.at[band, s], pair_in.at[band, s],
            pair_sum_send.at[band, s], pair_sum_recv.at[band, s], partner,
        )

    def along(band, source, target):
        return push(
            line_out.at[band, target], line_in.at[band, source],
            line_sum_send.at[band, target], line_sum_recv.at[band, source], target * PAIR + y,
        )

    def relay(k, band, s, rel, target):
        arrived(k, band, rel, s)
        sending(len(moves[k]), band, rel, s, target).start()
        moves[k].append((band, rel, s, target))

    def pair_sum(k, band, s):
        pair_out[band, s] = total[band, there(1, s)].astype(jnp.bfloat16)
        across(band, s).start()

    def line_sum(k, band, s):
        across(band, s).wait_recv()
        both = total[band, there(0, s)] + pair_in[band, s].astype(jnp.float32)
        line_out[band, s] = both.astype(jnp.bfloat16)
        along(band, k, s).start()

    def drain(k):
        for at, which in enumerate(moves[k]):
            sending(at, *which).wait_send()
        for band in range(bands):
            for s in range(length):
                across(band, s).wait_send()
                if s != k:
                    along(band, k, s).wait_send()

    def finish(k, band):
        across(band, k).wait_recv()
        sums = total[band, there(0, k)] + pair_in[band, k].astype(jnp.float32)
        for s in range(length):
            if s == k:
                continue
            along(band, s, k).wait_recv()
            sums = sums + line_in[band, s].astype(jnp.float32)
        here = pl.ds(band * rows, rows)
        dk_ref[here, :] = (sums[0] * HEAD_SIZE**-0.5).astype(jnp.bfloat16)
        dv_ref[here, :] = sums[1].astype(jnp.bfloat16)

    for at, peer in enumerate(peers):
        go(push(lens.at[me], lens.at[me], len_send.at[at], len_recv.at[me], peer))
    loads[0].wait()
    loads[1].wait()
    columns = group * rows
    lane_row = lax.rem(lax.broadcasted_iota(jnp.int32, (1, columns), 1), rows)
    starts = []

    def documents():
        for at, peer in enumerate(peers):
            push(
                lens.at[peer], lens.at[peer], len_send.at[at], len_recv.at[peer], peer
            ).wait_recv()
        running = jnp.zeros((1, lens.shape[-1]), jnp.int32)
        for b in range(shards):
            starts.append(jnp.concatenate([running] * (columns // lens.shape[-1]), axis=1))
            running = running + lens[b, 0:1, :]
        loads[2].wait()
        loads[3].wait()

    def compute(band, head):
        first = max(band - 1, 0)
        if head == 0:
            token = (band * rows + lane_row) * shards + me
            begin_at = jnp.zeros_like(token)
            for s in starts:
                begin_at = jnp.where(s <= token, s, begin_at)
            block = (band - first + 1, PAIR, length, rows, columns)
            iota = [lax.broadcasted_iota(jnp.int32, block, axis) for axis in range(4)]
            key_row = (first + iota[0]) * rows + iota[3]
            key_token = (key_row * shards + iota[2] * PAIR + iota[1]).reshape(-1, columns)
            masks[band] = (key_token <= token) & (key_token >= begin_at)
            each(lambda k: [arrived(k, band, rel, s) for rel in (0, 1) for s in range(length)] and None)
        attend((kv, q_buf, g_buf, attn_ref, dq_ref, total), me, band, head, masks[band], group)

    def act(k, step):
        kind, band, *which = step[0], *(int(digit) for digit in step[1:])
        flip = (lambda at: length - 1 - at) if k >= length // 2 else (lambda at: at)
        if kind == "s":
            s, rel, target = which
            relay(k, band, flip(s), rel, target if target == length else flip(target))
        elif kind == "p":
            pair_sum(k, band, flip(which[0]))
        elif kind == "l":
            line_sum(k, band, flip(which[0]))
        else:
            finish(k, band)

    masks = {}
    queues = [list(STEPS[0 if edge(k) else 1]) for k in range(length)]

    def pump(k):
        while queues[k] and queues[k][0][0] != "c":
            act(k, queues[k].pop(0))

    def begin(k):
        while queues[k][0][0] == "s" and queues[k][0][2:4] == ("00" if edge(k) else "10"):
            act(k, queues[k].pop(0))

    each(begin)
    while True:
        each(pump)
        if not queues[0]:
            break
        if not starts:
            documents()
        step = queues[0][0]
        for queue in queues:
            queue.pop(0)
        compute(int(step[1]), int(step[2]))
    for send in sends:
        send.wait_send()
    each(drain)


def hand_over(*refs):
    count = len(refs) // 2
    sems = refs[-1]
    copies = [
        pltpu.make_async_copy(refs[at], refs[count + at], sems.at[at]) for at in range(count)
    ]
    for copy in copies:
        copy.start()
    for copy in copies:
        copy.wait()


def per_device(query_states, key_states, value_state_array, grad_output, doc_lengths):
    shards = lax.axis_size("dp")
    row_count = query_states.shape[0]
    rows = SPAN // shards
    if rows % 16 or row_count % rows or shards != PAIR * LINE:
        return per_device_by_document(
            query_states, key_states, value_state_array, grad_output, doc_lengths
        )
    bands = row_count // rows
    width = key_states.shape[-1]
    wide = query_states.shape[-1]
    shape = jax.ShapeDtypeStruct
    flat = (row_count, wide)
    small = (row_count, width)
    length = shards // PAIR
    dma = pltpu.SemaphoreType.DMA
    def pinned(array):
        return pltpu.with_memory_space_constraint(array, pltpu.HBM)

    hbm = pl.BlockSpec(memory_space=pltpu.HBM)
    shapes = tuple(shape(dims, jnp.bfloat16) for dims in (flat, flat, small, small))
    results = pl.pallas_call(
        local_kernel,
        out_shape=shapes,
        in_specs=[pl.BlockSpec(memory_space=pltpu.SMEM)] + [hbm] * 4,
        out_specs=[pl.BlockSpec(memory_space=pltpu.VMEM)] * 4,
        scratch_shapes=[
            pltpu.VMEM((shards, 1, 128), jnp.int32),
            pltpu.VMEM((bands, shards, 2, rows, width), jnp.bfloat16),
            pltpu.VMEM(flat, jnp.bfloat16),
            pltpu.VMEM(flat, jnp.bfloat16),
            pltpu.VMEM((bands, shards, 2, rows, width), jnp.float32),
        ]
        + [pltpu.VMEM((bands, length, 2, rows, width), jnp.bfloat16)] * 4
        + [
            dma((4,)),
            dma((shards,)),
            dma((shards,)),
            dma((2 * bands * shards,)),
            dma((bands, shards)),
        ]
        + [dma((bands, length))] * 4,
        compiler_params=pltpu.CompilerParams(
            collective_id=0, has_side_effects=True, vmem_limit_bytes=48 << 20
        ),
    )(
        doc_lengths,
        pinned(query_states.reshape(flat)),
        pinned(key_states.reshape(bands, rows, width)),
        pinned(value_state_array.reshape(bands, rows, width)),
        pinned(grad_output.reshape(flat)),
    )
    results = pl.pallas_call(
        hand_over,
        out_shape=shapes,
        in_specs=[pl.BlockSpec(memory_space=pl.ANY)] * 4,
        out_specs=[hbm] * 4,
        scratch_shapes=[dma((4,))],
        compiler_params=pltpu.CompilerParams(vmem_limit_bytes=1 << 20),
    )(*results)
    return tuple(result[:, None, :] for result in results)


def solution(mesh):
    in_specs = (
        P(None, "dp", "mp"),
        P(None, "dp", "mp"),
        P(None, "dp", "mp"),
        P(None, "dp", "mp"),
        P("dp"),
    )
    out_specs = (P(None, "dp", "mp"), P(None, "dp", "mp"), P(None, "dp", "mp"), P(None, "dp", "mp"))
    return jax.shard_map(
        per_device, mesh=mesh, in_specs=in_specs, out_specs=out_specs, check_vma=False
    )
```
